512 devices in a mesh: dp: 8 (over z_hi, y), tm: 64 (over z_lo, x, core).
Axes of the slice: x: 4, y: 4, z: 16 (z_hi: 2, z_lo: 8; z = z_hi * 8 + z_lo), core: 2. Of those that a mesh axis runs over, the one named last changes fastest.
Arguments:
- query_proj: bfloat16 [8, 8192, 768], P('dp', 'tm'), may hold values from -240 to 240
- key_proj: bfloat16 [8, 8192, 768], P('dp', 'tm'), may hold values from -6 to 6
- value_proj: bfloat16 [8, 8192, 768], P('dp', 'tm'), may hold values from -6 to 6
- cotangent: bfloat16 [8, 8192, 768], P('dp', 'tm'), may hold values from -6 to 6
- lengths: int32 [8], P('dp'), may hold values from 4096 to 8192, as said below
- rel_bias: float32 [12, 257], replicated, may hold values from -4 to 4
Outputs:
- context: bfloat16 [8, 8192, 768], P('dp', 'tm')
- grad_query: bfloat16 [8, 8192, 768], P('dp', 'tm')
- grad_key: bfloat16 [8, 8192, 768], P('dp', 'tm')
- grad_value: bfloat16 [8, 8192, 768], P('dp', 'tm')
- grad_bias: float32 [12, 257], replicated
The draws below stay inside these ranges and needn't reach their ends.
Inputs may be any that keep to these rules, and one draw needn't show every extreme that they name: `lengths`: one utterance has all 8192 frames valid and another exactly 4096.
All inputs are finite; a program needn't handle non-finite values.
Results may differ from the reference program's by a relative error of at most 0.005.
Values may be sent and summed in bfloat16 or wider, within the bound.
No kernel may reach another device: no remote copies, remote signals or barrier semaphores. Data moves between devices by JAX's collectives and lax.ppermute only.
A program may use at most 64 MiB of HBM per device.

```python
import jax
import jax.numpy as jnp
from jax import lax

H = 12
HD = 64
W = 128
F = 128
D = 768
BATCH = 8
FRAMES = 8192
N_TM = 64


def drawn_pair(key):
    array_shape = (BATCH, FRAMES, D)
    key_drawn = jnp.clip(jax.random.normal(jax.random.fold_in(key, 21), array_shape, jnp.float32), -6.0, 6.0)
    query_drawn = jnp.clip(jax.random.normal(jax.random.fold_in(key, 22), array_shape, jnp.float32), -6.0, 6.0)
    return (query_drawn, key_drawn)


def draw_query_proj(key, part):
    return drawn_pair(key)[0].astype(jnp.bfloat16)


def draw_key_proj(key, part):
    return drawn_pair(key)[1].astype(jnp.bfloat16)


def draw_lengths(key, part):
    drawn = jax.random.randint(jax.random.fold_in(key, 11), (BATCH,), FRAMES // 2, FRAMES + 1)
    longest = jax.random.randint(jax.random.fold_in(key, 12), (), 0, BATCH)
    shortest = (longest + 1 + jax.random.randint(jax.random.fold_in(key, 13), (), 0, BATCH - 1)) % BATCH
    positions = jnp.arange(BATCH)
    drawn = jnp.where(positions == longest, FRAMES, drawn)
    drawn = jnp.where(positions == shortest, FRAMES // 2, drawn)
    return drawn.astype(jnp.int32)


def block_scale(own_key, shape, shards, low, largest):
    def one(axis_at, parts):
        heights = jax.random.uniform(jax.random.fold_in(jax.random.fold_in(own_key, 6), axis_at), (parts,), jnp.float32, low / len(shards), largest / len(shards))
        return jnp.repeat(jnp.exp(heights), shape[axis_at] // parts).reshape((-1,) + (1,) * (len(shape) - axis_at - 1))

    loudness = one(*shards[0])
    for cut in shards[1:]:
        loudness = loudness * one(*cut)
    return loudness


def noise(rng, shape, spread, limit, shards=(), kind=jnp.bfloat16):
    level = block_scale(rng, shape, shards, -0.22, 0.18) if shards else 1.0
    entries = jax.random.normal(rng, shape, jnp.float32) * spread * level
    return jnp.minimum(jnp.maximum(entries, -limit), limit).astype(kind)


def setup_inputs(seed: int = 0) -> dict:
    seeds = jax.random.split(jax.random.key(seed), 7)
    return {
        "query_proj": draw_query_proj(jax.random.fold_in(seeds[6], 71), 0),
        "key_proj": draw_key_proj(jax.random.fold_in(seeds[6], 71), 0),
        "value_proj": noise(seeds[2], (BATCH, FRAMES, D), 1.0, 6.0, ((0, 8), (1, 64))),
        "cotangent": noise(seeds[3], (BATCH, FRAMES, D), 1.0, 6.0, ((0, 8), (1, 64))),
        "lengths": draw_lengths(jax.random.fold_in(seeds[6], 71), 0),
        "rel_bias": noise(seeds[5], (H, 2 * W + 1), 1.0, 4.0, (), jnp.float32),
    }


masked_score = -1e30


def band_matrix(bias_table, height, breadth):
    num_heads = bias_table.shape[0]
    span_cols = bias_table.shape[1]
    repeated = jnp.broadcast_to(bias_table[:, None, :], (num_heads, height, span_cols))
    padded = jnp.pad(repeated, ((0, 0), (0, 0), (0, breadth + 1 - span_cols)))
    flattened = padded.reshape(num_heads, height * (breadth + 1))[:, : height * breadth]
    return flattened.reshape(num_heads, height, breadth)


def band_sum(values, span_cols):
    num_heads, height, breadth = values.shape
    flattened = jnp.pad(values.reshape(num_heads, height * breadth), ((0, 0), (0, height)))
    return jnp.sum(flattened.reshape(num_heads, height, breadth + 1)[:, :, :span_cols], axis=1)


def query_side(query_rows, key_rows, value_rows, grad_rows, bias_table, query_pos, key_pos, length):
    scaling = HD ** -0.5
    height = query_rows.shape[0]
    breadth = key_rows.shape[0]
    scores = jnp.einsum("qhd,khd->hqk", query_rows.astype(jnp.float32), key_rows.astype(jnp.float32)) * scaling
    scores = scores + band_matrix(bias_table, height, breadth)
    allowed = (jnp.abs(key_pos[None, :] - query_pos[:, None]) <= W) & (key_pos[None, :] >= 0) & (key_pos[None, :] < length)
    scores = jnp.where(allowed[None], scores, masked_score)
    row_max = jnp.max(scores, axis=-1)
    shifted = jnp.exp(scores - row_max[..., None])
    row_total = jnp.sum(shifted, axis=-1)
    log_total = row_max + jnp.log(row_total)
    attn_probs = shifted / row_total[..., None]
    valid_rows = query_pos < length
    probs_low = attn_probs.astype(jnp.bfloat16)
    mixed = jnp.einsum("hqk,khd->qhd", probs_low.astype(jnp.float32), value_rows.astype(jnp.float32))
    context = jnp.where(valid_rows[:, None, None], mixed, 0.0).astype(jnp.bfloat16)
    masked_grad = jnp.where(valid_rows[:, None, None], grad_rows, jnp.zeros_like(grad_rows))
    grad_probs = jnp.einsum("qhd,khd->hqk", masked_grad.astype(jnp.float32), value_rows.astype(jnp.float32))
    row_delta = jnp.sum(attn_probs * grad_probs, axis=-1)
    grad_scores = attn_probs * (grad_probs - row_delta[..., None])
    grad_low = grad_scores.astype(jnp.bfloat16)
    grad_query = (jnp.einsum("hqk,khd->qhd", grad_low.astype(jnp.float32), key_rows.astype(jnp.float32)) * scaling).astype(jnp.bfloat16)
    grad_table = band_sum(grad_scores, bias_table.shape[1])
    return context, grad_query, log_total, row_delta, grad_table


def key_side(key_rows, value_rows, query_rows, grad_rows, log_total, row_delta, bias_table, key_pos, query_pos, length):
    scaling = HD ** -0.5
    height = key_rows.shape[0]
    breadth = query_rows.shape[0]
    scores = jnp.einsum("khd,qhd->hkq", key_rows.astype(jnp.float32), query_rows.astype(jnp.float32)) * scaling
    scores = scores + band_matrix(bias_table[:, ::-1], height, breadth)
    valid_query = (query_pos >= 0) & (query_pos < length)
    allowed = (jnp.abs(query_pos[None, :] - key_pos[:, None]) <= W) & (key_pos[:, None] < length) & valid_query[None, :]
    attn_probs = jnp.where(allowed[None], jnp.exp(jnp.where(allowed[None], scores - log_total[:, None, :], 0.0)), 0.0)
    probs_low = attn_probs.astype(jnp.bfloat16)
    masked_grad = jnp.where(valid_query[:, None, None], grad_rows, jnp.zeros_like(grad_rows))
    grad_probs = jnp.einsum("khd,qhd->hkq", value_rows.astype(jnp.float32), masked_grad.astype(jnp.float32))
    grad_scores = attn_probs * (grad_probs - row_delta[:, None, :])
    grad_low = grad_scores.astype(jnp.bfloat16)
    grad_key = jnp.einsum("hkq,qhd->khd", grad_low.astype(jnp.float32), query_rows.astype(jnp.float32)) * scaling
    grad_value = jnp.einsum("hkq,qhd->khd", probs_low.astype(jnp.float32), masked_grad.astype(jnp.float32))
    return grad_key.astype(jnp.bfloat16), grad_value.astype(jnp.bfloat16)


def reference(query_proj, key_proj, value_proj, cotangent, lengths, rel_bias):
    extended = F + 2 * W
    blocks = BATCH * N_TM
    rim_pad = ((0, 0), (W, W), (0, 0))
    key_padded = jnp.pad(key_proj, rim_pad)
    value_padded = jnp.pad(value_proj, rim_pad)
    query_padded = jnp.pad(query_proj, rim_pad)
    grad_padded = jnp.pad(cotangent, rim_pad)
    zero_index = jnp.zeros((), jnp.int32)

    def forward_block(block_index):
        utterance = (block_index // N_TM).astype(jnp.int32)
        first_frame = ((block_index % N_TM) * F).astype(jnp.int32)
        length = lengths[utterance]
        query_rows = lax.dynamic_slice(query_proj, (utterance, first_frame, zero_index), (1, F, D))[0].reshape(F, H, HD)
        grad_rows = lax.dynamic_slice(cotangent, (utterance, first_frame, zero_index), (1, F, D))[0].reshape(F, H, HD)
        key_rows = lax.dynamic_slice(key_padded, (utterance, first_frame, zero_index), (1, extended, D))[0].reshape(extended, H, HD)
        value_rows = lax.dynamic_slice(value_padded, (utterance, first_frame, zero_index), (1, extended, D))[0].reshape(extended, H, HD)
        query_pos = first_frame + jnp.arange(F, dtype=jnp.int32)
        key_pos = first_frame - W + jnp.arange(extended, dtype=jnp.int32)
        return query_side(query_rows, key_rows, value_rows, grad_rows, rel_bias, query_pos, key_pos, length)

    context, grad_query, log_total, row_delta, grad_tables = lax.map(forward_block, jnp.arange(blocks, dtype=jnp.int32))
    context = context.reshape(BATCH, FRAMES, D)
    grad_query = grad_query.reshape(BATCH, FRAMES, D)
    grad_bias = jnp.sum(grad_tables, axis=0)
    log_total = jnp.pad(log_total.reshape(BATCH, N_TM, H, F).transpose(0, 2, 1, 3).reshape(BATCH, H, FRAMES), ((0, 0), (0, 0), (W, W)))
    row_delta = jnp.pad(row_delta.reshape(BATCH, N_TM, H, F).transpose(0, 2, 1, 3).reshape(BATCH, H, FRAMES), ((0, 0), (0, 0), (W, W)))

    def keyside_block(block_index):
        utterance = (block_index // N_TM).astype(jnp.int32)
        first_frame = ((block_index % N_TM) * F).astype(jnp.int32)
        length = lengths[utterance]
        key_rows = lax.dynamic_slice(key_proj, (utterance, first_frame, zero_index), (1, F, D))[0].reshape(F, H, HD)
        value_rows = lax.dynamic_slice(value_proj, (utterance, first_frame, zero_index), (1, F, D))[0].reshape(F, H, HD)
        query_rows = lax.dynamic_slice(query_padded, (utterance, first_frame, zero_index), (1, extended, D))[0].reshape(extended, H, HD)
        grad_rows = lax.dynamic_slice(grad_padded, (utterance, first_frame, zero_index), (1, extended, D))[0].reshape(extended, H, HD)
        total_rows = lax.dynamic_slice(log_total, (utterance, zero_index, first_frame), (1, H, extended))[0]
        delta_rows = lax.dynamic_slice(row_delta, (utterance, zero_index, first_frame), (1, H, extended))[0]
        key_pos = first_frame + jnp.arange(F, dtype=jnp.int32)
        query_pos = first_frame - W + jnp.arange(extended, dtype=jnp.int32)
        return key_side(key_rows, value_rows, query_rows, grad_rows, total_rows, delta_rows, rel_bias, key_pos, query_pos, length)

    grad_key, grad_value = lax.map(keyside_block, jnp.arange(blocks, dtype=jnp.int32))
    return context, grad_query, grad_key.reshape(BATCH, FRAMES, D), grad_value.reshape(BATCH, FRAMES, D), grad_bias
```

```python
import functools

import jax
import jax.numpy as jnp
from jax import lax
from jax.experimental import pallas as pl
from jax.experimental.pallas import tpu as pltpu
from jax.sharding import Mesh
from jax.sharding import PartitionSpec as P

H = 12
HD = 64
W = 128
F = 128
D = 768
PAIRS = 6
AXES = ("dp_0", "dp_1", "tm_0", "tm_1", "tm_2")
TM = ("tm_0", "tm_1", "tm_2")
DP = ("dp_0", "dp_1")
Z16 = ("dp_0", "tm_0")
X8 = ("tm_1", "tm_2")
Y4 = ("dp_1",)
NEG = -1e30
ROWS = 32
f32 = jnp.float32
bf16 = jnp.bfloat16

NT = (((1,), (1,)), ((), ()))
NN = (((1,), (0,)), ((), ()))


def dot(a, b, dims=NN):
    return lax.dot_general(a, b, dims, preferred_element_type=f32)


def attention_kernel(
    info, q_ref, g_ref, k_ref, v_ref, left_ref, right_ref, rt_ref, t0_ref,
    ctx_ref, dq_ref, dk_ref, dv_ref, dl_ref, dr_ref, gb_ref, acc_ref, diag_ref,
):
    pair = pl.program_id(0)
    first, length = info[0], info[1]
    row = lax.broadcasted_iota(jnp.int32, (F, F), 0)
    lane = lax.broadcasted_iota(jnp.int32, (F, F), 1)
    low = lane < HD
    valid = (first + row) < length
    zero = jnp.zeros((F, F), bf16)

    q = q_ref[...] * jnp.asarray(HD**-0.5, bf16)
    g = jnp.where(valid, g_ref[...], zero)
    q2 = jnp.concatenate([jnp.where(low, q, zero), jnp.where(low, zero, q)], axis=0)
    g2 = jnp.concatenate([jnp.where(low, g, zero), jnp.where(low, zero, g)], axis=0)
    keys = (left_ref[0], k_ref[...], right_ref[0])
    values = (left_ref[1], v_ref[...], right_ref[1])

    below = lane < row
    on = lane == row
    biases = ([], [], [])
    for h in range(2):
        head = 2 * pair + h
        u0 = pltpu.roll(jnp.broadcast_to(rt_ref[2 * head], (F, F)), 0, 1, stride=1, stride_axis=0)
        u1 = pltpu.roll(jnp.broadcast_to(rt_ref[2 * head + 1], (F, F)), 0, 1, stride=1, stride_axis=0)
        biases[0].append(jnp.where(below, u0, jnp.where(on, jnp.broadcast_to(t0_ref[head], (F, F)), NEG)))
        biases[1].append(jnp.where(below, u1, u0))
        biases[2].append(jnp.where(below, NEG, u1))

    scores = []
    for a in range(3):
        pos = first + (a - 1) * W + lax.broadcasted_iota(jnp.int32, (F, 2 * F), 0)
        s = dot(keys[a], q2, NT) + jnp.concatenate(biases[a], axis=1)
        scores.append(jnp.where((pos >= 0) & (pos < length), s, NEG))
    top = functools.reduce(jnp.maximum, [jnp.max(s, axis=0, keepdims=True) for s in scores])
    exps = [jnp.exp(s - top) for s in scores]
    total = functools.reduce(jnp.add, [jnp.sum(e, axis=0, keepdims=True) for e in exps])
    inverse = 1.0 / total
    probs = [e * inverse for e in exps]
    gp = [dot(v, g2, NT) for v in values]
    delta = functools.reduce(jnp.add, [jnp.sum(p * d, axis=0, keepdims=True) for p, d in zip(probs, gp)])
    ds = [p * (d - delta) for p, d in zip(probs, gp)]
    p_low = [p.astype(bf16) for p in probs]
    ds_low = [d.astype(bf16) for d in ds]

    ctx_t = sum(dot(jnp.transpose(v), p) for v, p in zip(values, p_low))
    dq_t = sum(dot(jnp.transpose(k), d) for k, d in zip(keys, ds_low))
    ctx = jnp.transpose(jnp.concatenate([ctx_t[:HD, :F], ctx_t[HD:, F:]], axis=0))
    ctx_ref[...] = jnp.where(valid, ctx, 0.0).astype(bf16)
    dq = jnp.transpose(jnp.concatenate([dq_t[:HD, :F], dq_t[HD:, F:]], axis=0))
    dq_ref[...] = (dq * (HD**-0.5)).astype(bf16)

    dk_ref[...] = dot(ds_low[1], q2)
    dv_ref[...] = dot(p_low[1], g2)
    dl_ref[0] = dot(ds_low[0], q2).astype(bf16)
    dl_ref[1] = dot(p_low[0], g2).astype(bf16)
    dr_ref[0] = dot(ds_low[2], q2).astype(bf16)
    dr_ref[1] = dot(p_low[2], g2).astype(bf16)

    for h in range(2):
        part = [d[:, h * F : (h + 1) * F] for d in ds]
        y1 = jnp.where(below, part[0], part[1])
        y2 = jnp.where(below, part[1], part[2])
        y3 = jnp.where(on, part[0], 0.0)
        for y, ref, at in ((y1, acc_ref, 2 * pair + h), (y2, acc_ref, H + 2 * pair + h)):
            total_y = y[:8]
            for k in range(1, 16):
                total_y = total_y + pltpu.roll(y[8 * k : 8 * k + 8], F - 8 * k, 1)
            ref[at] = total_y
        diag_ref[2 * pair + h] = jnp.sum(y3, axis=0, keepdims=True)

    @pl.when(pair == PAIRS - 1)
    def _():
        summed = acc_ref[:, 0, :]
        for s in range(1, 8):
            summed = summed + pltpu.roll(acc_ref[:, s, :], F - s, 1)
        l0 = lax.broadcasted_iota(jnp.int32, (F, F), 0)
        flip = jnp.where((l0 + lane == F) | ((l0 == 0) & (lane == 0)), 1.0, 0.0).astype(f32)
        turned = lax.dot_general(summed, flip, NN, precision=lax.Precision.HIGHEST, preferred_element_type=f32)
        at0 = lax.broadcasted_iota(jnp.int32, (H, F), 1) == 0
        zed = jnp.sum(diag_ref[:, 0, :], axis=1, keepdims=True)
        one, two = turned[:H], turned[H:]
        gb_ref[:H] = jnp.where(at0, zed, one)
        gb_ref[H : 2 * H] = jnp.where(at0, one[:, :1], two)
        spot = lax.broadcasted_iota(jnp.int32, (H, F), 0) == lax.broadcasted_iota(jnp.int32, (H, F), 1)
        last = jnp.sum(jnp.where(spot, two[:, :1], 0.0), axis=0, keepdims=True)
        gb_ref[2 * H :] = jnp.broadcast_to(last, (ROWS - 2 * H, F))


def attention(info, q, g, k, v, left, right, rt, t0):
    tile = pl.BlockSpec((F, F), lambda p, *_: (0, p))
    both = pl.BlockSpec((2, F, F), lambda p, *_: (0, 0, p))
    whole = lambda shape: pl.BlockSpec(shape, lambda p, *_: (0,) * len(shape))
    return pl.pallas_call(
        attention_kernel,
        grid_spec=pltpu.PrefetchScalarGridSpec(
            num_scalar_prefetch=1,
            grid=(PAIRS,),
            in_specs=[tile, tile, tile, tile, both, both, whole((2 * H, 1, F)), whole((H, 1, F))],
            out_specs=[tile, tile, tile, tile, both, both, whole((ROWS, F))],
            scratch_shapes=[pltpu.VMEM((2 * H, 8, F), f32), pltpu.VMEM((H, 1, F), f32)],
        ),
        out_shape=[
            jax.ShapeDtypeStruct((F, D), bf16),
            jax.ShapeDtypeStruct((F, D), bf16),
            jax.ShapeDtypeStruct((F, D), f32),
            jax.ShapeDtypeStruct((F, D), f32),
            jax.ShapeDtypeStruct((2, F, D), bf16),
            jax.ShapeDtypeStruct((2, F, D), bf16),
            jax.ShapeDtypeStruct((ROWS, F), f32),
        ],
        name="attention",
    )(info, q, g, k, v, left, right, rt, t0)


def assemble_kernel(z_ref, out_ref):
    total = jnp.sum(z_ref[...].astype(f32), axis=0)
    out_ref[:, :F] = total[:H]
    out_ref[:, F : 2 * F] = total[H : 2 * H]
    spot = lax.broadcasted_iota(jnp.int32, (H, F), 0) == lax.broadcasted_iota(jnp.int32, (H, F), 1)
    out_ref[:, 2 * F :] = jnp.sum(jnp.where(spot, total[2 * H : 2 * H + 1], 0.0), axis=1, keepdims=True)


def assemble(z):
    return pl.pallas_call(
        assemble_kernel, out_shape=jax.ShapeDtypeStruct((H, 2 * W + 1), f32), name="assemble"
    )(z)


def exchange(y, axes, dtype):
    count = 1
    for axis in axes:
        count *= lax.axis_size(axis)
    sent = jnp.broadcast_to(y.astype(dtype)[None], (count,) + y.shape)
    return lax.all_to_all(sent, axes, 0, 0, tiled=True)


def on_device(query_proj, key_proj, value_proj, cotangent, lengths, rel_bias):
    first = lax.axis_index(TM) * F
    info = jnp.stack([first.astype(jnp.int32), lengths[0]])
    ends = lax.axis_size(TM) - 1
    ahead = [(i, i + 1) for i in range(ends)]
    back = [(i + 1, i) for i in range(ends)]
    kv = jnp.concatenate([key_proj, value_proj], axis=0)
    left = lax.ppermute(kv, TM, ahead)
    right = lax.ppermute(kv, TM, back)
    rt = rel_bias[:, :0:-1].reshape(H, 2, F)[:, ::-1].reshape(2 * H, 1, F)
    t0 = jnp.broadcast_to(rel_bias[:, :1, None], (H, 1, F))
    ctx, dq, dk, dv, dl, dr, gb = attention(
        info, query_proj[0], cotangent[0], key_proj[0], value_proj[0], left, right, rt, t0
    )
    from_right = lax.ppermute(dl, TM, back)
    from_left = lax.ppermute(dr, TM, ahead)
    z = exchange(gb, Z16, bf16)
    z = exchange(jnp.sum(z.astype(f32), axis=0), X8, f32)
    z = exchange(jnp.sum(z, axis=0), Y4, f32)
    grad_bias = assemble(z)
    both = from_right.astype(f32) + from_left.astype(f32)
    grad_key = (dk + both[0]).astype(bf16)
    grad_value = (dv + both[1]).astype(bf16)
    return ctx[None], dq[None], grad_key[None], grad_value[None], grad_bias


def solution(mesh):
    finer = Mesh(mesh.devices.reshape(2, 4, 8, 4, 2), AXES)
    in_specs = (P(DP, TM, None), P(DP, TM, None), P(DP, TM, None), P(DP, TM, None), P(DP), P())
    out_specs = (P(DP, TM, None), P(DP, TM, None), P(DP, TM, None), P(DP, TM, None), P())
    return jax.shard_map(
        on_device, mesh=finer, in_specs=in_specs, out_specs=out_specs, check_vma=False
    )
```

```python
import functools

import jax
import jax.numpy as jnp
from jax import lax
from jax.experimental import pallas as pl
from jax.experimental.pallas import tpu as pltpu
from jax.sharding import Mesh
from jax.sharding import PartitionSpec as P


H = 12
HD = 64
W = 128
F = 128
D = 768
PAIRS = 6
AXES = ("dp_0", "dp_1", "tm_0", "tm_1", "tm_2")
TM = ("tm_0", "tm_1", "tm_2")
DP = ("dp_0", "dp_1")
Z16 = ("dp_0", "tm_0")
XY = ("dp_1", "tm_1", "tm_2")
NEG = -1e30
ROWS = 32
SCALE = HD**-0.5
UNROLL = (6, 6, 6)
f32 = jnp.float32
bf16 = jnp.bfloat16

NT = (((1,), (1,)), ((), ()))
NN = (((1,), (0,)), ((), ()))


def dot(a, b, dims=NN):
    return lax.dot_general(a, b, dims, preferred_element_type=f32)


def grids():
    row = lax.broadcasted_iota(jnp.int32, (F, F), 0)
    lane = lax.broadcasted_iota(jnp.int32, (F, F), 1)
    return row, lane


def flip_matrix():
    row, lane = grids()
    return jnp.where((row + lane == F) | ((row == 0) & (lane == 0)), 1.0, 0.0).astype(f32)


def flip(rows):
    return lax.dot_general(
        rows, flip_matrix(), NN, precision=lax.Precision.HIGHEST, preferred_element_type=f32
    )


def stacked(info, q, g):
    row, lane = grids()
    low = lane < HD
    zero = jnp.zeros((F, F), bf16)
    q = q * jnp.asarray(SCALE, bf16)
    g = jnp.where(info[0] + row < info[1], g, zero)
    q2 = jnp.concatenate([jnp.where(low, q, zero), jnp.where(low, zero, q)], axis=0)
    g2 = jnp.concatenate([jnp.where(low, g, zero), jnp.where(low, zero, g)], axis=0)
    return q2, g2


def masked_below(bias, start, length):
    pos = start + lax.broadcasted_iota(jnp.int32, bias.shape, 0)
    return jnp.where((pos >= 0) & (pos < length), bias, NEG)


def lanes(pair):
    return pl.ds(pl.multiple_of(pair * F, F), F)


def own_kernel(
    info, q_hbm, g_hbm, table_hbm, kv_ref, s_ref, gp_ref, bias_ref, qg_ref, rt_ref, table_ref, sem
):
    fetch((q_hbm, g_hbm, table_hbm), (qg_ref.at[0], qg_ref.at[1], table_ref), sem)
    first, length, odd = info[0], info[1], info[2]
    row, lane = grids()
    low, high, end = table_ref[:, :F], table_ref[:, F : 2 * F], table_ref[:, 2 * F :]
    at0 = lax.broadcasted_iota(jnp.int32, (H, F), 1) == 0
    rt_ref[0] = jnp.where(at0, high[:, :1], flip(low))
    rt_ref[1] = jnp.where(at0, end, flip(high))
    rt_ref[2] = jnp.broadcast_to(low[:, :1], (H, F))
    below, on = lane < row, lane == row

    def step(pair, carry):
        at = lanes(pair)
        q2, g2 = stacked(info, qg_ref[0, :, at], qg_ref[1, :, at])
        before, own, after = [], [], []
        for h in range(2):
            spread = lambda which: jnp.broadcast_to(rt_ref[which, pl.ds(2 * pair + h, 1), :], (F, F))
            u0 = pltpu.roll(spread(0), 0, 1, stride=1, stride_axis=0)
            u1 = pltpu.roll(spread(1), 0, 1, stride=1, stride_axis=0)
            before.append(jnp.where(below, u0, jnp.where(on, spread(2), NEG)))
            own.append(jnp.where(below, u1, u0))
            after.append(jnp.where(below, NEG, u1))
        before, own, after = (jnp.concatenate(b, axis=1) for b in (before, own, after))
        bias_ref[1 - odd, pair] = masked_below(before, first - W, length)
        bias_ref[odd, pair] = masked_below(after, first + W, length)
        s_ref[pair] = dot(kv_ref[0, :, at], q2, NT) + masked_below(own, first, length)
        gp_ref[pair] = dot(kv_ref[1, :, at], g2, NT)
        return carry

    lax.fori_loop(0, PAIRS, step, 0, unroll=UNROLL[0])


def rows_kernel(
    info, a_ref, b_ref, s_ref, gp_ref, bias_ref, qg_ref, p_ref, ds_ref, gb_ref, acc_ref, diag_ref,
):
    odd = info[2] == 1
    row, lane = grids()
    below, on = lane < row, lane == row

    def step(pair, carry):
        at = lanes(pair)
        q2, g2 = stacked(info, qg_ref[0, :, at], qg_ref[1, :, at])
        scores = [
            dot(a_ref[0, :, at], q2, NT) + bias_ref[0, pair],
            s_ref[pair],
            dot(b_ref[0, :, at], q2, NT) + bias_ref[1, pair],
        ]
        top = functools.reduce(jnp.maximum, [jnp.max(s, axis=0, keepdims=True) for s in scores])
        exps = [jnp.exp(s - top) for s in scores]
        total = functools.reduce(jnp.add, [jnp.sum(e, axis=0, keepdims=True) for e in exps])
        inverse = 1.0 / total
        probs = [e * inverse for e in exps]
        gp = [dot(a_ref[1, :, at], g2, NT), gp_ref[pair], dot(b_ref[1, :, at], g2, NT)]
        delta = functools.reduce(
            jnp.add, [jnp.sum(p * d, axis=0, keepdims=True) for p, d in zip(probs, gp)]
        )
        ds = [p * (d - delta) for p, d in zip(probs, gp)]
        for i in range(3):
            p_ref[pair, i * F : (i + 1) * F] = probs[i].astype(bf16)
            ds_ref[pair, i * F : (i + 1) * F] = ds[i].astype(bf16)
        for h in range(2):
            side_a, mid, side_b = (d[:, h * F : (h + 1) * F] for d in ds)
            before = jnp.where(odd, side_a, side_b)
            after = jnp.where(odd, side_b, side_a)
            y1 = jnp.where(below, before, mid)
            y2 = jnp.where(below, mid, after)
            for y, spot in ((y1, 2 * pair + h), (y2, H + 2 * pair + h)):
                total_y = y[:8]
                for k in range(1, 16):
                    total_y = total_y + pltpu.roll(y[8 * k : 8 * k + 8], F - 8 * k, 1)
                acc_ref[spot] = total_y
            diag_ref[2 * pair + h] = jnp.sum(jnp.where(on, before, 0.0), axis=0, keepdims=True)
        return carry

    lax.fori_loop(0, PAIRS, step, 0, unroll=UNROLL[1])
    summed = acc_ref[:, 0, :]
    for s in range(1, 8):
        summed = summed + pltpu.roll(acc_ref[:, s, :], F - s, 1)
    turned = flip(summed)
    head = lax.broadcasted_iota(jnp.int32, (H, F), 0)
    at = lax.broadcasted_iota(jnp.int32, (H, F), 1)
    zed = jnp.sum(diag_ref[:, 0, :], axis=1, keepdims=True)
    one, two = turned[:H], turned[H:]
    last = jnp.sum(jnp.where(head == at, two[:, :1], 0.0), axis=0, keepdims=True)
    packed = jnp.concatenate(
        [
            jnp.where(at == 0, zed, one),
            jnp.where(at == 0, one[:, :1], two),
            jnp.broadcast_to(last, (ROWS - 2 * H, F)),
        ],
        axis=0,
    ).astype(bf16)
    for i in range(gb_ref.shape[0]):
        gb_ref[i] = packed


def outputs_kernel(
    info, q_hbm, g_hbm, k_hbm, v_hbm, a_hbm, b_hbm, p_ref, ds_ref,
    ctx_ref, dq_ref, dk_ref, dv_ref, da_ref, db_ref, held, a_ref, b_ref, sem,
):
    fetch(
        (q_hbm, g_hbm, k_hbm, v_hbm, a_hbm, b_hbm),
        [held.at[i] for i in range(4)] + [a_ref, b_ref],
        sem,
    )
    row, _ = grids()
    valid = info[0] + row < info[1]

    def step(pair, carry):
        at = lanes(pair)
        q2, g2 = stacked(info, held[0, :, at], held[1, :, at])
        p, ds = p_ref[pair], ds_ref[pair]
        keys = jnp.concatenate([a_ref[0, :, at], held[2, :, at], b_ref[0, :, at]], axis=0)
        values = jnp.concatenate([a_ref[1, :, at], held[3, :, at], b_ref[1, :, at]], axis=0)
        dk = dot(ds, q2)
        dv = dot(p, g2)
        da_ref[0, :, at] = dk[:F].astype(bf16)
        da_ref[1, :, at] = dv[:F].astype(bf16)
        dk_ref[:, at] = dk[F : 2 * F]
        dv_ref[:, at] = dv[F : 2 * F]
        db_ref[0, :, at] = dk[2 * F :].astype(bf16)
        db_ref[1, :, at] = dv[2 * F :].astype(bf16)
        ctx_t = dot(jnp.transpose(values), p)
        dq_t = dot(jnp.transpose(keys), ds)
        ctx = jnp.transpose(jnp.concatenate([ctx_t[:HD, :F], ctx_t[HD:, F:]], axis=0))
        ctx_ref[:, at] = jnp.where(valid, ctx, 0.0).astype(bf16)
        dq = jnp.transpose(jnp.concatenate([dq_t[:HD, :F], dq_t[HD:, F:]], axis=0))
        dq_ref[:, at] = (dq * SCALE).astype(bf16)
        return carry

    lax.fori_loop(0, PAIRS, step, 0, unroll=UNROLL[2])


def fetch(sources, targets, sem):
    copies = [
        pltpu.make_async_copy(source, target, sem.at[i])
        for i, (source, target) in enumerate(zip(sources, targets))
    ]
    for copy in copies:
        copy.start()
    for copy in copies:
        copy.wait()


def stack_kernel(k_ref, v_ref, out_ref, sem):
    fetch((k_ref, v_ref), (out_ref.at[0], out_ref.at[1]), sem)


def stack(k, v):
    return pl.pallas_call(
        stack_kernel,
        in_specs=[pl.BlockSpec(memory_space=pltpu.HBM)] * 2,
        out_specs=pl.BlockSpec(memory_space=pltpu.VMEM),
        out_shape=shape(bf16, 2, F, D),
        scratch_shapes=[pltpu.SemaphoreType.DMA((2,))],
        compiler_params=pltpu.CompilerParams(vmem_limit_bytes=1 << 20),
        name="stack",
    )(k, v)


def in_vmem(kernel, far, args, out_shape, scratch, flops):
    vmem = pl.BlockSpec(memory_space=pltpu.VMEM)
    hbm = pl.BlockSpec(memory_space=pltpu.HBM)
    return pl.pallas_call(
        kernel,
        in_specs=[pl.BlockSpec(memory_space=pltpu.SMEM)]
        + [hbm] * far
        + [vmem] * (len(args) - 1 - far),
        out_specs=[vmem] * len(out_shape),
        out_shape=out_shape,
        scratch_shapes=scratch,
        compiler_params=pltpu.CompilerParams(vmem_limit_bytes=16 << 20),
        cost_estimate=pl.CostEstimate(flops=flops, bytes_accessed=4 << 20, transcendentals=0),
    )(*args)


def shape(dtype, *dims):
    return jax.ShapeDtypeStruct(dims, dtype)


def own_part(*args):
    return in_vmem(
        own_kernel, 3, args,
        [shape(f32, PAIRS, F, 2 * F)] * 2
        + [shape(f32, 2, PAIRS, F, 2 * F), shape(bf16, 2, F, D)],
        [
            pltpu.VMEM((3, H, F), f32),
            pltpu.VMEM((H, 2 * W + 1), f32),
            pltpu.SemaphoreType.DMA((3,)),
        ],
        1 << 30,
    )


def row_part(copies, *args):
    return in_vmem(
        rows_kernel, 0, args,
        [shape(bf16, PAIRS, 3 * F, 2 * F)] * 2 + [shape(bf16, copies, ROWS, F)],
        [pltpu.VMEM((2 * H, 8, F), f32), pltpu.VMEM((H, 1, F), f32)], 1 << 30,
    )


def output_part(*args):
    return in_vmem(
        outputs_kernel, 6, args,
        [shape(bf16, F, D)] * 2 + [shape(f32, F, D)] * 2 + [shape(bf16, 2, F, D)] * 2,
        [pltpu.VMEM((4, F, D), bf16)]
        + [pltpu.VMEM((2, F, D), bf16)] * 2
        + [pltpu.SemaphoreType.DMA((6,))],
        1 << 30,
    )


def finish_kernel(dk_ref, dv_ref, a_ref, b_ref, gk_ref, gv_ref):
    for i, (own, out) in enumerate(((dk_ref, gk_ref), (dv_ref, gv_ref))):
        out[...] = (own[...] + a_ref[i].astype(f32) + b_ref[i].astype(f32)).astype(bf16)


def finish(dk, dv, a, b):
    vmem = pl.BlockSpec(memory_space=pltpu.VMEM)
    return pl.pallas_call(
        finish_kernel,
        in_specs=[vmem] * 4,
        out_shape=[shape(bf16, F, D)] * 2,
        compiler_params=pltpu.CompilerParams(vmem_limit_bytes=16 << 20),
        name="finish",
    )(dk, dv, a, b)


def size_of(axes):
    count = 1
    for axis in axes:
        count *= lax.axis_size(axis)
    return count


def step(query_proj, key_proj, value_proj, cotangent, lengths, rel_bias):
    ends = size_of(TM)
    at = lax.axis_index(TM)
    info = jnp.stack([at * F, lengths[0], at & 1]).astype(jnp.int32)
    near = [(i, i ^ 1) for i in range(ends)]
    far = [(i, i + 1 if i % 2 else i - 1) for i in range(1, ends - 1)]
    stay = lambda x: pltpu.with_memory_space_constraint(x, pltpu.HBM)
    q, k, v, g = (stay(x[0]) for x in (query_proj, key_proj, value_proj, cotangent))
    rel_bias = stay(rel_bias)
    kv = stack(k, v)
    side_b = lax.ppermute(kv, TM, far)
    side_a = lax.ppermute(kv, TM, near)
    s, gp, bias, qg = own_part(info, q, g, rel_bias, kv)
    p, ds, gb = row_part(size_of(Z16), info, side_a, side_b, s, gp, bias, qg)
    z = lax.all_to_all(gb, Z16, 0, 0, tiled=True)
    ctx, dq, dk, dv, da, db = output_part(info, q, g, k, v, stay(side_a), stay(side_b), p, ds)
    from_b = lax.ppermute(db, TM, far)
    from_a = lax.ppermute(da, TM, near)
    z = jnp.sum(z.astype(f32), axis=0).astype(bf16)
    z = jnp.broadcast_to(z[None], (size_of(XY), ROWS, F))
    z = lax.all_to_all(z, XY, 0, 0, tiled=True)
    z = jnp.sum(z.astype(f32), axis=0)
    grad_bias = jnp.concatenate([z[:H], z[H : 2 * H], z[2 * H, :H, None]], axis=1)
    grad_key, grad_value = finish(dk, dv, from_a, from_b)
    return ctx[None], dq[None], grad_key[None], grad_value[None], grad_bias


def solution(mesh):
    finer = Mesh(mesh.devices.reshape(2, 4, 8, 4, 2), AXES)
    in_specs = (P(DP, TM, None), P(DP, TM, None), P(DP, TM, None), P(DP, TM, None), P(DP), P())
    out_specs = (P(DP, TM, None), P(DP, TM, None), P(DP, TM, None), P(DP, TM, None), P())
    return jax.shard_map(step, mesh=finer, in_specs=in_specs, out_specs=out_specs, check_vma=False)
```

```python
import jax
import jax.numpy as jnp
from jax import lax
from jax.experimental import pallas as pl
from jax.experimental.pallas import tpu as pltpu
from jax.sharding import Mesh
from jax.sharding import PartitionSpec as P


H = 12
HD = 64
W = 128
F = 128
D = 768
PAIRS = 6
AXES = ("dp_0", "dp_1", "tm_0", "tm_1", "tm_2")
TM = ("tm_0", "tm_1", "tm_2")
DP = ("dp_0", "dp_1")
Z16 = ("dp_0", "tm_0")
XY = ("dp_1", "tm_1", "tm_2")
NEG = -1e30
ROWS = 32
SCALE = HD**-0.5
f32 = jnp.float32
bf16 = jnp.bfloat16

NT = (((1,), (1,)), ((), ()))
NN = (((1,), (0,)), ((), ()))


def dot(a, b, dims=NN):
    return lax.dot_general(a, b, dims, preferred_element_type=f32)


def grids():
    row = lax.broadcasted_iota(jnp.int32, (F, F), 0)
    lane = lax.broadcasted_iota(jnp.int32, (F, F), 1)
    return row, lane


def flip_matrix():
    row, lane = grids()
    return jnp.where((row + lane == F) | ((row == 0) & (lane == 0)), 1.0, 0.0).astype(f32)


def flip(rows):
    return lax.dot_general(
        rows, flip_matrix(), NN, precision=lax.Precision.HIGHEST, preferred_element_type=f32
    )


def position(length_ref):
    at = lax.axis_index(TM)
    return at * F, length_ref[0], at & 1


def stacked(info, q, g):
    row, lane = grids()
    low = lane < HD
    zero = jnp.zeros((F, F), bf16)
    q = q * jnp.asarray(SCALE, bf16)
    g = jnp.where(info[0] + row < info[1], g, zero)
    q2 = jnp.concatenate([jnp.where(low, q, zero), jnp.where(low, zero, q)], axis=0)
    g2 = jnp.concatenate([jnp.where(low, g, zero), jnp.where(low, zero, g)], axis=0)
    return q2, g2


def lanes(pair):
    return pl.ds(pl.multiple_of(pair * F, F), F)


def twice(x):
    return jnp.concatenate([x, x], axis=1)


def own_kernel(
    length_ref, q_hbm, g_hbm, k_hbm, v_hbm, table_hbm,
    s_ref, gp_ref, bias_ref, edge_ref, qg_ref, rt_ref, table_ref, kv_ref, sem,
):
    fetch(
        (q_hbm, g_hbm, k_hbm, v_hbm, table_hbm),
        (qg_ref.at[0], qg_ref.at[1], kv_ref.at[0], kv_ref.at[1], table_ref),
        sem,
    )
    info = position(length_ref)
    first, length = info[0], info[1]
    row, lane = grids()
    low, high, end = table_ref[:, :F], table_ref[:, F : 2 * F], table_ref[:, 2 * F :]
    at0 = lax.broadcasted_iota(jnp.int32, (H, F), 1) == 0
    rt_ref[0] = jnp.where(at0, high[:, :1], flip(low))
    rt_ref[1] = jnp.where(at0, end, flip(high))
    rt_ref[2] = jnp.broadcast_to(low[:, :1], (H, F))
    below = lane < row
    here = (first + row) < length
    around = jnp.where(below, first - W + row, first + W + row)
    around = (around >= 0) & (around < length)
    edge = first - W + lane[:1]
    edge = (edge >= 0) & (edge < length)

    def step(pair, carry):
        at = lanes(pair)
        q2, g2 = stacked(info, qg_ref[0, :, at], qg_ref[1, :, at])
        own, other, ends = [], [], []
        for h in range(2):
            line = lambda which: rt_ref[which, pl.ds(2 * pair + h, 1), :]
            spread = lambda which: jnp.broadcast_to(line(which), (F, F))
            u0 = pltpu.roll(spread(0), 0, 1, stride=1, stride_axis=0)
            u1 = pltpu.roll(spread(1), 0, 1, stride=1, stride_axis=0)
            own.append(jnp.where(here, jnp.where(below, u1, u0), NEG))
            other.append(jnp.where(around, jnp.where(below, u0, u1), NEG))
            ends.append(jnp.where(edge, line(2), NEG))
        bias_ref[pair] = jnp.concatenate(other, axis=1)
        edge_ref[pair] = jnp.concatenate(ends, axis=1)
        s_ref[pair] = dot(kv_ref[0, :, at], q2, NT) + jnp.concatenate(own, axis=1)
        gp_ref[pair] = dot(kv_ref[1, :, at], g2, NT)
        return carry

    lax.fori_loop(0, PAIRS, step, 0, unroll=PAIRS)


def rows_kernel(
    length_ref, ak_ref, av_ref, bk_ref, bv_ref, s_ref, gp_ref, bias_ref, edge_ref, qg_ref,
    p_ref, ds_ref, p0_ref, ds0_ref, gb_ref, acc_ref,
):
    info = position(length_ref)
    row, lane = grids()
    below, on = lane < row, lane == row
    below2, on2 = twice(below), twice(on)

    def run(before_refs, after_refs):
        for pair in range(PAIRS):
            at = pl.ds(pair * F, F)
            q2, g2 = stacked(info, qg_ref[0, :, at], qg_ref[1, :, at])

            def around(which, rows2):
                left = dot(before_refs[which][:, at], rows2, NT)
                right = dot(after_refs[which][:, at], rows2, NT)
                edge = jnp.sum(jnp.where(on2, left, 0.0), axis=0, keepdims=True)
                return jnp.where(below2, left, right), edge

            s1, s0 = around(0, q2)
            s1, s0, s2 = s1 + bias_ref[pair], s0 + edge_ref[pair], s_ref[pair]
            top = jnp.maximum(jnp.max(jnp.maximum(s1, s2), axis=0, keepdims=True), s0)
            e0, e1, e2 = jnp.exp(s0 - top), jnp.exp(s1 - top), jnp.exp(s2 - top)
            inverse = 1.0 / (e0 + jnp.sum(e1 + e2, axis=0, keepdims=True))
            p0, p1, p2 = e0 * inverse, e1 * inverse, e2 * inverse
            g1, g0 = around(1, g2)
            g2_own = gp_ref[pair]
            delta = p0 * g0 + jnp.sum(p1 * g1 + p2 * g2_own, axis=0, keepdims=True)
            d0, d1, d2 = p0 * (g0 - delta), p1 * (g1 - delta), p2 * (g2_own - delta)
            p_ref[pair, 0], p_ref[pair, 1] = p1.astype(bf16), p2.astype(bf16)
            ds_ref[pair, 0], ds_ref[pair, 1] = d1.astype(bf16), d2.astype(bf16)
            p0_ref[pair], ds0_ref[pair] = p0, d0
            for h in range(2):
                part = slice(h * F, (h + 1) * F)
                y1 = jnp.where(below, d1[:, part], d2[:, part])
                y2 = jnp.where(below, d2[:, part], d1[:, part])
                for y, spot in ((y1, 2 * pair + h), (y2, H + 2 * pair + h)):
                    total_y = y[:8]
                    for k in range(1, 16):
                        total_y = total_y + pltpu.roll(y[8 * k : 8 * k + 8], F - 8 * k, 1)
                    acc_ref[spot] = total_y

    @pl.when(info[2] == 1)
    def _():
        run((ak_ref, av_ref), (bk_ref, bv_ref))

    @pl.when(info[2] == 0)
    def _():
        run((bk_ref, bv_ref), (ak_ref, av_ref))

    summed = acc_ref[:, 0, :]
    for s in range(1, 8):
        summed = summed + pltpu.roll(acc_ref[:, s, :], F - s, 1)
    turned = flip(summed)
    head = lax.broadcasted_iota(jnp.int32, (H, F), 0)
    at = lax.broadcasted_iota(jnp.int32, (H, F), 1)
    edges = ds0_ref[:, 0, :]
    zed = jnp.concatenate(
        [
            jnp.sum(edges[pair : pair + 1, h * F : (h + 1) * F], axis=1, keepdims=True)
            for pair in range(PAIRS)
            for h in range(2)
        ],
        axis=0,
    )
    one, two = turned[:H], turned[H:]
    last = jnp.sum(jnp.where(head == at, two[:, :1], 0.0), axis=0, keepdims=True)
    packed = jnp.concatenate(
        [
            jnp.where(at == 0, zed, one),
            jnp.where(at == 0, one[:, :1], two),
            jnp.broadcast_to(last, (ROWS - 2 * H, F)),
        ],
        axis=0,
    ).astype(bf16)
    for i in range(gb_ref.shape[0]):
        gb_ref[i] = packed


def unfolded(pair_ref, edge_ref, pair, below2, on2):
    folded = pair_ref[pair, 0]
    zero = jnp.zeros_like(folded)
    edge = jnp.broadcast_to(edge_ref[pair], folded.shape).astype(bf16)
    before = jnp.where(below2, folded, jnp.where(on2, edge, zero))
    return before, jnp.where(below2, zero, folded)


def sides_kernel(
    length_ref, q_hbm, g_hbm, p_ref, ds_ref, p0_ref, ds0_ref, da_ref, db_ref, held, sem,
):
    fetch((q_hbm, g_hbm), [held.at[i] for i in range(2)], sem)
    info = position(length_ref)
    row, lane = grids()
    below2, on2 = twice(lane < row), twice(lane == row)

    def run(*refs):
        for pair in range(PAIRS):
            at = pl.ds(pair * F, F)
            q2, g2 = stacked(info, held[0, :, at], held[1, :, at])
            dk = dot(jnp.concatenate(unfolded(ds_ref, ds0_ref, pair, below2, on2), axis=0), q2)
            dv = dot(jnp.concatenate(unfolded(p_ref, p0_ref, pair, below2, on2), axis=0), g2)
            for i, ref in enumerate(refs):
                ref[0, :, at] = dk[i * F : (i + 1) * F].astype(bf16)
                ref[1, :, at] = dv[i * F : (i + 1) * F].astype(bf16)

    @pl.when(info[2] == 1)
    def _():
        run(da_ref, db_ref)

    @pl.when(info[2] == 0)
    def _():
        run(db_ref, da_ref)


def outputs_kernel(
    length_ref, q_hbm, g_hbm, k_hbm, v_hbm, ak_hbm, av_hbm, bk_hbm, bv_hbm,
    p_ref, ds_ref, p0_ref, ds0_ref, fa_ref, fb_ref,
    ctx_ref, dq_ref, gk_ref, gv_ref, held, qg_ref, sem,
):
    info = position(length_ref)
    odd = info[2]
    fetch(
        (q_hbm, g_hbm, k_hbm, v_hbm, ak_hbm, av_hbm, bk_hbm, bv_hbm),
        [qg_ref.at[0], qg_ref.at[1], held.at[1, 0], held.at[1, 1]]
        + [held.at[2 - 2 * odd, i] for i in range(2)]
        + [held.at[2 * odd, i] for i in range(2)],
        sem,
    )
    row, lane = grids()
    below2, on2 = twice(lane < row), twice(lane == row)
    valid = info[0] + row < info[1]
    for pair in range(PAIRS):
        at = pl.ds(pair * F, F)
        q2, g2 = stacked(info, qg_ref[0, :, at], qg_ref[1, :, at])
        p, ds = p_ref[pair, 1], ds_ref[pair, 1]
        for i, (own, out) in enumerate(((dot(ds, q2), gk_ref), (dot(p, g2), gv_ref))):
            total = own + fa_ref[i, :, at].astype(f32) + fb_ref[i, :, at].astype(f32)
            out[:, at] = total.astype(bf16)
        p_before, p_after = unfolded(p_ref, p0_ref, pair, below2, on2)
        ds_before, ds_after = unfolded(ds_ref, ds0_ref, pair, below2, on2)
        keys = jnp.concatenate([held[i, 0, :, at] for i in range(3)], axis=0)
        values = jnp.concatenate([held[i, 1, :, at] for i in range(3)], axis=0)
        ctx_t = dot(jnp.transpose(values), jnp.concatenate([p_before, p, p_after], axis=0))
        dq_t = dot(jnp.transpose(keys), jnp.concatenate([ds_before, ds, ds_after], axis=0))
        ctx = jnp.transpose(jnp.concatenate([ctx_t[:HD, :F], ctx_t[HD:, F:]], axis=0))
        ctx_ref[:, at] = jnp.where(valid, ctx, 0.0).astype(bf16)
        dq = jnp.transpose(jnp.concatenate([dq_t[:HD, :F], dq_t[HD:, F:]], axis=0))
        dq_ref[:, at] = (dq * SCALE).astype(bf16)


def fetch(sources, targets, sem):
    copies = [
        pltpu.make_async_copy(source, target, sem.at[i])
        for i, (source, target) in enumerate(zip(sources, targets))
    ]
    for copy in copies:
        copy.start()
    for copy in copies:
        copy.wait()


def in_vmem(kernel, far, args, out_shape, scratch, flops):
    vmem = pl.BlockSpec(memory_space=pltpu.VMEM)
    hbm = pl.BlockSpec(memory_space=pltpu.HBM)
    return pl.pallas_call(
        kernel,
        in_specs=[pl.BlockSpec(memory_space=pltpu.SMEM)]
        + [hbm] * far
        + [vmem] * (len(args) - 1 - far),
        out_specs=[vmem] * len(out_shape),
        out_shape=out_shape,
        scratch_shapes=scratch,
        compiler_params=pltpu.CompilerParams(vmem_limit_bytes=16 << 20),
        cost_estimate=pl.CostEstimate(flops=flops, bytes_accessed=4 << 20, transcendentals=0),
    )(*args)


def shape(dtype, *dims):
    return jax.ShapeDtypeStruct(dims, dtype)


def own_part(*args):
    return in_vmem(
        own_kernel, 5, args,
        [shape(f32, PAIRS, F, 2 * F)] * 3
        + [shape(f32, PAIRS, 1, 2 * F), shape(bf16, 2, F, D)],
        [
            pltpu.VMEM((3, H, F), f32),
            pltpu.VMEM((H, 2 * W + 1), f32),
            pltpu.VMEM((2, F, D), bf16),
            pltpu.SemaphoreType.DMA((5,)),
        ],
        1 << 30,
    )


def row_part(copies, *args):
    return in_vmem(
        rows_kernel, 0, args,
        [shape(bf16, PAIRS, 2, F, 2 * F)] * 2
        + [shape(f32, PAIRS, 1, 2 * F)] * 2
        + [shape(bf16, copies, ROWS, F)],
        [pltpu.VMEM((2 * H, 8, F), f32)], 1 << 30,
    )


def side_part(*args):
    return in_vmem(
        sides_kernel, 2, args,
        [shape(bf16, 2, F, D)] * 2,
        [pltpu.VMEM((2, F, D), bf16), pltpu.SemaphoreType.DMA((2,))], 1 << 30,
    )


def output_part(*args):
    return in_vmem(
        outputs_kernel, 8, args,
        [shape(bf16, F, D)] * 4,
        [
            pltpu.VMEM((3, 2, F, D), bf16),
            pltpu.VMEM((2, F, D), bf16),
            pltpu.SemaphoreType.DMA((8,)),
        ],
        1 << 30,
    )


def size_of(axes):
    count = 1
    for axis in axes:
        count *= lax.axis_size(axis)
    return count


def step(query_proj, key_proj, value_proj, cotangent, lengths, rel_bias):
    ends = size_of(TM)
    near = [(i, i ^ 1) for i in range(ends)]
    far = [(i, i + 1 if i % 2 else i - 1) for i in range(1, ends - 1)]
    stay = lambda x: pltpu.with_memory_space_constraint(x, pltpu.HBM)
    q, k, v, g = (stay(x[0]) for x in (query_proj, key_proj, value_proj, cotangent))
    table = stay(rel_bias)
    bk = lax.ppermute(key_proj[0], TM, far)
    bv = lax.ppermute(value_proj[0], TM, far)
    ak = lax.ppermute(key_proj[0], TM, near)
    av = lax.ppermute(value_proj[0], TM, near)
    s, gp, bias, edge, qg = own_part(lengths, q, g, k, v, table)
    p, ds, p0, ds0, gb = row_part(
        size_of(Z16), lengths, ak, av, bk, bv, s, gp, bias, edge, qg
    )
    z = lax.all_to_all(gb, Z16, 0, 0, tiled=True)
    da, db = side_part(lengths, q, g, p, ds, p0, ds0)
    fb = lax.ppermute(db, TM, far)
    fa = lax.ppermute(da, TM, near)
    z = jnp.sum(z.astype(f32), axis=0).astype(bf16)
    z = jnp.broadcast_to(z[None], (size_of(XY), ROWS, F))
    z = lax.all_to_all(z, XY, 0, 0, tiled=True)
    ctx, dq, grad_key, grad_value = output_part(
        lengths, q, g, k, v, stay(ak), stay(av), stay(bk), stay(bv), p, ds, p0, ds0, fa, fb
    )
    z = jnp.sum(z.astype(f32), axis=0)
    grad_bias = jnp.concatenate([z[:H], z[H : 2 * H], z[2 * H, :H, None]], axis=1)
    return ctx[None], dq[None], grad_key[None], grad_value[None], grad_bias


def solution(mesh):
    finer = Mesh(mesh.devices.reshape(2, 4, 8, 4, 2), AXES)
    in_specs = (P(DP, TM, None), P(DP, TM, None), P(DP, TM, None), P(DP, TM, None), P(DP), P())
    out_specs = (P(DP, TM, None), P(DP, TM, None), P(DP, TM, None), P(DP, TM, None), P())
    return jax.shard_map(step, mesh=finer, in_specs=in_specs, out_specs=out_specs, check_vma=False)
```

```python
import jax
import jax.numpy as jnp
from jax import lax
from jax.experimental import pallas as pl
from jax.experimental.pallas import tpu as pltpu
from jax.sharding import Mesh
from jax.sharding import PartitionSpec as P


H = 12
HD = 64
W = 128
F = 128
D = 768
PAIRS = 6
AXES = ("dp_0", "dp_1", "tm_0", "tm_1", "tm_2")
TM = ("tm_0", "tm_1", "tm_2")
DP = ("dp_0", "dp_1")
Z16 = ("dp_0", "tm_0")
XY = ("dp_1", "tm_1", "tm_2")
NEG = -1e30
ROWS = 32
SCALE = HD**-0.5
f32 = jnp.float32
bf16 = jnp.bfloat16

NT = (((1,), (1,)), ((), ()))
NN = (((1,), (0,)), ((), ()))


def dot(a, b, dims=NN):
    return lax.dot_general(a, b, dims, preferred_element_type=f32)


def grids():
    row = lax.broadcasted_iota(jnp.int32, (F, F), 0)
    lane = lax.broadcasted_iota(jnp.int32, (F, F), 1)
    return row, lane


def flip_matrix():
    row, lane = grids()
    return jnp.where((row + lane == F) | ((row == 0) & (lane == 0)), 1.0, 0.0).astype(f32)


def flip(rows):
    return lax.dot_general(
        rows, flip_matrix(), NN, precision=lax.Precision.HIGHEST, preferred_element_type=f32
    )


def position(length_ref):
    at = lax.axis_index(TM)
    return at * F, length_ref[0], at & 1


def stacked(info, q, g):
    row, lane = grids()
    low = lane < HD
    zero = jnp.zeros((F, F), bf16)
    q = q * jnp.asarray(SCALE, bf16)
    g = jnp.where(info[0] + row < info[1], g, zero)
    q2 = jnp.concatenate([jnp.where(low, q, zero), jnp.where(low, zero, q)], axis=0)
    g2 = jnp.concatenate([jnp.where(low, g, zero), jnp.where(low, zero, g)], axis=0)
    return q2, g2


def lanes(pair):
    return pl.ds(pl.multiple_of(pair * F, F), F)


def twice(x):
    return jnp.concatenate([x, x], axis=1)


def own_kernel(
    length_ref, q_hbm, g_hbm, table_hbm, kv_ref,
    s_ref, gp_ref, bias_ref, edge_ref, q2_ref, g2_ref, rt_ref, table_ref, qg_ref, sem,
):
    fetch((q_hbm, g_hbm, table_hbm), (qg_ref.at[0], qg_ref.at[1], table_ref), sem)
    info = position(length_ref)
    first, length = info[0], info[1]
    row, lane = grids()
    low, high, end = table_ref[:, :F], table_ref[:, F : 2 * F], table_ref[:, 2 * F :]
    at0 = lax.broadcasted_iota(jnp.int32, (H, F), 1) == 0
    rt_ref[0] = jnp.where(at0, high[:, :1], flip(low))
    rt_ref[1] = jnp.where(at0, end, flip(high))
    rt_ref[2] = jnp.broadcast_to(low[:, :1], (H, F))
    below = lane < row
    here = (first + row) < length
    around = jnp.where(below, first - W + row, first + W + row)
    around = (around >= 0) & (around < length)
    edge = first - W + lane[:1]
    edge = (edge >= 0) & (edge < length)

    def step(pair, carry):
        at = lanes(pair)
        q2, g2 = stacked(info, qg_ref[0, :, at], qg_ref[1, :, at])
        q2_ref[pair], g2_ref[pair] = q2, g2
        own, other, ends = [], [], []
        for h in range(2):
            line = lambda which: rt_ref[which, pl.ds(2 * pair + h, 1), :]
            spread = lambda which: jnp.broadcast_to(line(which), (F, F))
            u0 = pltpu.roll(spread(0), 0, 1, stride=1, stride_axis=0)
            u1 = pltpu.roll(spread(1), 0, 1, stride=1, stride_axis=0)
            own.append(jnp.where(here, jnp.where(below, u1, u0), NEG))
            other.append(jnp.where(around, jnp.where(below, u0, u1), NEG))
            ends.append(jnp.where(edge, line(2), NEG))
        bias_ref[pair] = jnp.concatenate(other, axis=1)
        edge_ref[pair] = jnp.concatenate(ends, axis=1)
        s_ref[pair] = dot(kv_ref[0, :, at], q2, NT) + jnp.concatenate(own, axis=1)
        gp_ref[pair] = dot(kv_ref[1, :, at], g2, NT)
        return carry

    lax.fori_loop(0, PAIRS, step, 0, unroll=PAIRS)


def rows_kernel(
    length_ref, a_ref, b_ref, s_ref, gp_ref, bias_ref, edge_ref, q2_ref, g2_ref,
    p_ref, ds_ref, p0_ref, ds0_ref, gb_ref, acc_ref,
):
    info = position(length_ref)
    row, lane = grids()
    below, on = lane < row, lane == row
    below2, on2 = twice(below), twice(on)
    hit = twice(lane & 7 == row)[:8]

    def run(before_ref, after_ref):
        for pair in range(PAIRS):
            at = pl.ds(pair * F, F)

            def around(which, rows2):
                left = dot(before_ref[which, :, at], rows2, NT)
                right = dot(after_ref[which, :, at], rows2, NT)
                edge = jnp.zeros((8, 2 * F), f32)
                for k in range(16):
                    edge = jnp.where(on2[8 * k : 8 * k + 8], left[8 * k : 8 * k + 8], edge)
                edge = jnp.sum(jnp.where(hit, edge, 0.0), axis=0, keepdims=True)
                return jnp.where(below2, left, right), edge

            s1, s0 = around(0, q2_ref[pair])
            s1, s0, s2 = s1 + bias_ref[pair], s0 + edge_ref[pair], s_ref[pair]
            top = jnp.maximum(jnp.max(jnp.maximum(s1, s2), axis=0, keepdims=True), s0)
            e0, e1, e2 = jnp.exp(s0 - top), jnp.exp(s1 - top), jnp.exp(s2 - top)
            g1, g0 = around(1, g2_ref[pair])
            g2 = gp_ref[pair]
            inverse = 1.0 / (e0 + jnp.sum(e1 + e2, axis=0, keepdims=True))
            delta = (e0 * g0 + jnp.sum(e1 * g1 + e2 * g2, axis=0, keepdims=True)) * inverse
            p0, p1, p2 = e0 * inverse, e1 * inverse, e2 * inverse
            d0, d1, d2 = p0 * (g0 - delta), p1 * (g1 - delta), p2 * (g2 - delta)
            p_ref[pair, 0], p_ref[pair, 1] = p1.astype(bf16), p2.astype(bf16)
            ds_ref[pair, 0], ds_ref[pair, 1] = d1.astype(bf16), d2.astype(bf16)
            p0_ref[pair], ds0_ref[pair] = p0, d0
            for h in range(2):
                part = slice(h * F, (h + 1) * F)
                y1 = jnp.where(below, d1[:, part], d2[:, part])
                y2 = jnp.where(below, d2[:, part], d1[:, part])
                for y, spot in ((y1, 2 * pair + h), (y2, H + 2 * pair + h)):
                    total_y = y[:8]
                    for k in range(1, 16):
                        total_y = total_y + pltpu.roll(y[8 * k : 8 * k + 8], F - 8 * k, 1)
                    acc_ref[spot] = total_y

    @pl.when(info[2] == 1)
    def _():
        run(a_ref, b_ref)

    @pl.when(info[2] == 0)
    def _():
        run(b_ref, a_ref)

    summed = acc_ref[:, 0, :]
    for s in range(1, 8):
        summed = summed + pltpu.roll(acc_ref[:, s, :], F - s, 1)
    turned = flip(summed)
    head = lax.broadcasted_iota(jnp.int32, (H, F), 0)
    at = lax.broadcasted_iota(jnp.int32, (H, F), 1)
    edges = ds0_ref[:, 0, :]
    zed = jnp.concatenate(
        [
            jnp.sum(edges[pair : pair + 1, h * F : (h + 1) * F], axis=1, keepdims=True)
            for pair in range(PAIRS)
            for h in range(2)
        ],
        axis=0,
    )
    one, two = turned[:H], turned[H:]
    last = jnp.sum(jnp.where(head == at, two[:, :1], 0.0), axis=0, keepdims=True)
    packed = jnp.concatenate(
        [
            jnp.where(at == 0, zed, one),
            jnp.where(at == 0, one[:, :1], two),
            jnp.broadcast_to(last, (ROWS - 2 * H, F)),
        ],
        axis=0,
    ).astype(bf16)
    for i in range(gb_ref.shape[0]):
        gb_ref[i] = packed


def unfolded(pair_ref, edge_ref, pair, below2, on2):
    folded = pair_ref[pair, 0]
    zero = jnp.zeros_like(folded)
    edge = jnp.broadcast_to(edge_ref[pair], folded.shape).astype(bf16)
    before = jnp.where(below2, folded, jnp.where(on2, edge, zero))
    return before, jnp.where(below2, zero, folded)


def sides_kernel(
    length_ref, q_hbm, g_hbm, p_ref, ds_ref, p0_ref, ds0_ref, da_ref, db_ref, held, sem,
):
    fetch((q_hbm, g_hbm), [held.at[i] for i in range(2)], sem)
    info = position(length_ref)
    row, lane = grids()
    below2, on2 = twice(lane < row), twice(lane == row)

    def run(*refs):
        for pair in range(PAIRS):
            at = pl.ds(pair * F, F)
            q2, g2 = stacked(info, held[0, :, at], held[1, :, at])
            dk = dot(jnp.concatenate(unfolded(ds_ref, ds0_ref, pair, below2, on2), axis=0), q2)
            dv = dot(jnp.concatenate(unfolded(p_ref, p0_ref, pair, below2, on2), axis=0), g2)
            for i, ref in enumerate(refs):
                ref[0, :, at] = dk[i * F : (i + 1) * F].astype(bf16)
                ref[1, :, at] = dv[i * F : (i + 1) * F].astype(bf16)

    @pl.when(info[2] == 1)
    def _():
        run(da_ref, db_ref)

    @pl.when(info[2] == 0)
    def _():
        run(db_ref, da_ref)


def outputs_kernel(
    length_ref, q_hbm, g_hbm, k_hbm, v_hbm, a_hbm, b_hbm,
    p_ref, ds_ref, p0_ref, ds0_ref, fa_ref, fb_ref,
    ctx_ref, dq_ref, gk_ref, gv_ref, held, qg_ref, sem,
):
    info = position(length_ref)
    odd = info[2]
    fetch(
        (q_hbm, g_hbm, k_hbm, v_hbm, a_hbm, b_hbm),
        [qg_ref.at[0], qg_ref.at[1], held.at[1, 0], held.at[1, 1]]
        + [held.at[2 - 2 * odd], held.at[2 * odd]],
        sem,
    )
    row, lane = grids()
    below2, on2 = twice(lane < row), twice(lane == row)
    valid = info[0] + row < info[1]
    for pair in range(PAIRS):
        at = pl.ds(pair * F, F)
        q2, g2 = stacked(info, qg_ref[0, :, at], qg_ref[1, :, at])
        p, ds = p_ref[pair, 1], ds_ref[pair, 1]
        for i, (own, out) in enumerate(((dot(ds, q2), gk_ref), (dot(p, g2), gv_ref))):
            total = own + fa_ref[i, :, at].astype(f32) + fb_ref[i, :, at].astype(f32)
            out[:, at] = total.astype(bf16)
        p_before, p_after = unfolded(p_ref, p0_ref, pair, below2, on2)
        ds_before, ds_after = unfolded(ds_ref, ds0_ref, pair, below2, on2)
        keys = jnp.concatenate([held[i, 0, :, at] for i in range(3)], axis=0)
        values = jnp.concatenate([held[i, 1, :, at] for i in range(3)], axis=0)
        ctx_t = dot(jnp.transpose(values), jnp.concatenate([p_before, p, p_after], axis=0))
        dq_t = dot(jnp.transpose(keys), jnp.concatenate([ds_before, ds, ds_after], axis=0))
        ctx = jnp.transpose(jnp.concatenate([ctx_t[:HD, :F], ctx_t[HD:, F:]], axis=0))
        ctx_ref[:, at] = jnp.where(valid, ctx, 0.0).astype(bf16)
        dq = jnp.transpose(jnp.concatenate([dq_t[:HD, :F], dq_t[HD:, F:]], axis=0))
        dq_ref[:, at] = (dq * SCALE).astype(bf16)


def fetch(sources, targets, sem):
    copies = [
        pltpu.make_async_copy(source, target, sem.at[i])
        for i, (source, target) in enumerate(zip(sources, targets))
    ]
    for copy in copies:
        copy.start()
    for copy in copies:
        copy.wait()


def stack_kernel(k_hbm, v_hbm, out_ref, sem):
    fetch((k_hbm, v_hbm), (out_ref.at[0], out_ref.at[1]), sem)


def stack(k, v):
    return pl.pallas_call(
        stack_kernel,
        in_specs=[pl.BlockSpec(memory_space=pltpu.HBM)] * 2,
        out_specs=pl.BlockSpec(memory_space=pltpu.VMEM),
        out_shape=shape(bf16, 2, F, D),
        scratch_shapes=[pltpu.SemaphoreType.DMA((2,))],
        compiler_params=pltpu.CompilerParams(vmem_limit_bytes=1 << 20),
        name="stack",
    )(k, v)


def in_vmem(kernel, far, args, out_shape, scratch, flops):
    vmem = pl.BlockSpec(memory_space=pltpu.VMEM)
    hbm = pl.BlockSpec(memory_space=pltpu.HBM)
    return pl.pallas_call(
        kernel,
        in_specs=[pl.BlockSpec(memory_space=pltpu.SMEM)]
        + [hbm] * far
        + [vmem] * (len(args) - 1 - far),
        out_specs=[vmem] * len(out_shape),
        out_shape=out_shape,
        scratch_shapes=scratch,
        compiler_params=pltpu.CompilerParams(vmem_limit_bytes=16 << 20),
        cost_estimate=pl.CostEstimate(flops=flops, bytes_accessed=4 << 20, transcendentals=0),
    )(*args)


def shape(dtype, *dims):
    return jax.ShapeDtypeStruct(dims, dtype)


def own_part(*args):
    return in_vmem(
        own_kernel, 3, args,
        [shape(f32, PAIRS, F, 2 * F)] * 3
        + [shape(f32, PAIRS, 1, 2 * F)]
        + [shape(bf16, PAIRS, 2 * F, F)] * 2,
        [
            pltpu.VMEM((3, H, F), f32),
            pltpu.VMEM((H, 2 * W + 1), f32),
            pltpu.VMEM((2, F, D), bf16),
            pltpu.SemaphoreType.DMA((3,)),
        ],
        1 << 30,
    )


def row_part(copies, *args):
    return in_vmem(
        rows_kernel, 0, args,
        [shape(bf16, PAIRS, 2, F, 2 * F)] * 2
        + [shape(f32, PAIRS, 1, 2 * F)] * 2
        + [shape(bf16, copies, ROWS, F)],
        [pltpu.VMEM((2 * H, 8, F), f32)], 1 << 30,
    )


def side_part(*args):
    return in_vmem(
        sides_kernel, 2, args,
        [shape(bf16, 2, F, D)] * 2,
        [pltpu.VMEM((2, F, D), bf16), pltpu.SemaphoreType.DMA((2,))], 1 << 30,
    )


def output_part(*args):
    return in_vmem(
        outputs_kernel, 6, args,
        [shape(bf16, F, D)] * 4,
        [
            pltpu.VMEM((3, 2, F, D), bf16),
            pltpu.VMEM((2, F, D), bf16),
            pltpu.SemaphoreType.DMA((6,)),
        ],
        1 << 30,
    )


def size_of(axes):
    count = 1
    for axis in axes:
        count *= lax.axis_size(axis)
    return count


def step(query_proj, key_proj, value_proj, cotangent, lengths, rel_bias):
    ends = size_of(TM)
    near = [(i, i ^ 1) for i in range(ends)]
    far = [(i, i + 1 if i % 2 else i - 1) for i in range(1, ends - 1)]
    stay = lambda x: pltpu.with_memory_space_constraint(x, pltpu.HBM)
    q, k, v, g = (stay(x[0]) for x in (query_proj, key_proj, value_proj, cotangent))
    table = stay(rel_bias)
    kv = stack(k, v)
    side_b = lax.ppermute(kv, TM, far)
    side_a = lax.ppermute(kv, TM, near)
    s, gp, bias, edge, q2, g2 = own_part(lengths, q, g, table, kv)
    p, ds, p0, ds0, gb = row_part(size_of(XY), lengths, side_a, side_b, s, gp, bias, edge, q2, g2)
    z = lax.all_to_all(gb, XY, 0, 0, tiled=True)
    da, db = side_part(lengths, q, g, p, ds, p0, ds0)
    fb = lax.ppermute(db, TM, far)
    fa = lax.ppermute(da, TM, near)
    z = jnp.sum(z.astype(f32), axis=0).astype(bf16)
    z = jnp.broadcast_to(z[None], (size_of(Z16), ROWS, F))
    z = lax.all_to_all(z, Z16, 0, 0, tiled=True)
    ctx, dq, grad_key, grad_value = output_part(
        lengths, q, g, k, v, stay(side_a), stay(side_b), p, ds, p0, ds0, fa, fb
    )
    z = jnp.sum(z.astype(f32), axis=0)
    grad_bias = jnp.concatenate([z[:H], z[H : 2 * H], z[2 * H, :H, None]], axis=1)
    return ctx[None], dq[None], grad_key[None], grad_value[None], grad_bias


def solution(mesh):
    finer = Mesh(mesh.devices.reshape(2, 4, 8, 4, 2), AXES)
    in_specs = (P(DP, TM, None), P(DP, TM, None), P(DP, TM, None), P(DP, TM, None), P(DP), P())
    out_specs = (P(DP, TM, None), P(DP, TM, None), P(DP, TM, None), P(DP, TM, None), P())
    return jax.shard_map(step, mesh=finer, in_specs=in_specs, out_specs=out_specs, check_vma=False)
```

```python
import jax
import jax.numpy as jnp
from jax import lax
from jax.experimental import pallas as pl
from jax.experimental.pallas import tpu as pltpu
from jax.sharding import Mesh
from jax.sharding import PartitionSpec as P


H = 12
HD = 64
W = 128
F = 128
D = 768
PAIRS = 6
AXES = ("dp_0", "dp_1", "tm_0", "tm_1", "tm_2")
TM = ("tm_0", "tm_1", "tm_2")
DP = ("dp_0", "dp_1")
Z16 = ("dp_0", "tm_0")
XY = ("dp_1", "tm_1", "tm_2")
NEG = -1e30
ROWS = 32
HEAD_XY = 23
HEAD_Z = 10
SCALE = HD**-0.5
f32 = jnp.float32
bf16 = jnp.bfloat16

NT = (((1,), (1,)), ((), ()))
NN = (((1,), (0,)), ((), ()))


def dot(a, b, dims=NN):
    return lax.dot_general(a, b, dims, preferred_element_type=f32)


def grids():
    row = lax.broadcasted_iota(jnp.int32, (F, F), 0)
    lane = lax.broadcasted_iota(jnp.int32, (F, F), 1)
    return row, lane


def flip_matrix():
    row, lane = grids()
    return jnp.where((row + lane == F) | ((row == 0) & (lane == 0)), 1.0, 0.0).astype(f32)


def flip(rows):
    return lax.dot_general(
        rows, flip_matrix(), NN, precision=lax.Precision.HIGHEST, preferred_element_type=f32
    )


def position(length_ref):
    at = lax.axis_index(TM)
    return at * F, length_ref[0], at & 1


def stacked(info, q, g):
    row, lane = grids()
    low = lane < HD
    zero = jnp.zeros((F, F), bf16)
    q = q * jnp.asarray(SCALE, bf16)
    g = jnp.where(info[0] + row < info[1], g, zero)
    q2 = jnp.concatenate([jnp.where(low, q, zero), jnp.where(low, zero, q)], axis=0)
    g2 = jnp.concatenate([jnp.where(low, g, zero), jnp.where(low, zero, g)], axis=0)
    return q2, g2


def lanes(pair):
    return pl.ds(pl.multiple_of(pair * F, F), F)


def twice(x):
    return jnp.concatenate([x, x], axis=1)


def own_kernel(
    length_ref, q_hbm, g_hbm, table_hbm, kv_ref,
    s_ref, gp_ref, bias_ref, edge_ref, q2_ref, g2_ref, rt_ref, table_ref, qg_ref, sem,
):
    fetch((q_hbm, g_hbm, table_hbm), (qg_ref.at[0], qg_ref.at[1], table_ref), sem)
    info = position(length_ref)
    first, length = info[0], info[1]
    row, lane = grids()
    low, high, end = table_ref[:, :F], table_ref[:, F : 2 * F], table_ref[:, 2 * F :]
    at0 = lax.broadcasted_iota(jnp.int32, (H, F), 1) == 0
    rt_ref[0] = jnp.where(at0, high[:, :1], flip(low))
    rt_ref[1] = jnp.where(at0, end, flip(high))
    rt_ref[2] = jnp.broadcast_to(low[:, :1], (H, F))
    below = lane < row
    here = (first + row) < length
    around = jnp.where(below, first - W + row, first + W + row)
    around = (around >= 0) & (around < length)
    edge = first - W + lane[:1]
    edge = (edge >= 0) & (edge < length)

    def step(pair, carry):
        at = lanes(pair)
        q2, g2 = stacked(info, qg_ref[0, :, at], qg_ref[1, :, at])
        q2_ref[pair], g2_ref[pair] = q2, g2
        own, other, ends = [], [], []
        for h in range(2):
            line = lambda which: rt_ref[which, pl.ds(2 * pair + h, 1), :]
            spread = lambda which: jnp.broadcast_to(line(which), (F, F))
            u0 = pltpu.roll(spread(0), 0, 1, stride=1, stride_axis=0)
            u1 = pltpu.roll(spread(1), 0, 1, stride=1, stride_axis=0)
            own.append(jnp.where(here, jnp.where(below, u1, u0), NEG))
            other.append(jnp.where(around, jnp.where(below, u0, u1), NEG))
            ends.append(jnp.where(edge, line(2), NEG))
        bias_ref[pair] = jnp.concatenate(other, axis=1)
        edge_ref[pair] = jnp.concatenate(ends, axis=1)
        s_ref[pair] = dot(kv_ref[0, :, at], q2, NT) + jnp.concatenate(own, axis=1)
        gp_ref[pair] = dot(kv_ref[1, :, at], g2, NT)
        return carry

    lax.fori_loop(0, PAIRS, step, 0, unroll=PAIRS)


def rows_kernel(
    length_ref, a_ref, b_ref, s_ref, gp_ref, bias_ref, edge_ref, q2_ref, g2_ref,
    p_ref, ds_ref, p0_ref, ds0_ref, gb_ref, acc_ref,
):
    info = position(length_ref)
    row, lane = grids()
    below, on = lane < row, lane == row
    below2, on2 = twice(below), twice(on)
    hit = twice(lane & 7 == row)[:8]

    def run(before_ref, after_ref):
        for pair in range(PAIRS):
            at = pl.ds(pair * F, F)

            def around(which, rows2):
                left = dot(before_ref[which, :, at], rows2, NT)
                right = dot(after_ref[which, :, at], rows2, NT)
                edge = jnp.zeros((8, 2 * F), f32)
                for k in range(16):
                    edge = jnp.where(on2[8 * k : 8 * k + 8], left[8 * k : 8 * k + 8], edge)
                edge = jnp.sum(jnp.where(hit, edge, 0.0), axis=0, keepdims=True)
                return jnp.where(below2, left, right), edge

            s1, s0 = around(0, q2_ref[pair])
            s1, s0, s2 = s1 + bias_ref[pair], s0 + edge_ref[pair], s_ref[pair]
            top = jnp.maximum(jnp.max(jnp.maximum(s1, s2), axis=0, keepdims=True), s0)
            e0, e1, e2 = jnp.exp(s0 - top), jnp.exp(s1 - top), jnp.exp(s2 - top)
            g1, g0 = around(1, g2_ref[pair])
            g2 = gp_ref[pair]
            inverse = 1.0 / (e0 + jnp.sum(e1 + e2, axis=0, keepdims=True))
            delta = (e0 * g0 + jnp.sum(e1 * g1 + e2 * g2, axis=0, keepdims=True)) * inverse
            p0, p1, p2 = e0 * inverse, e1 * inverse, e2 * inverse
            d0, d1, d2 = p0 * (g0 - delta), p1 * (g1 - delta), p2 * (g2 - delta)
            p_ref[pair, 0], p_ref[pair, 1] = p1.astype(bf16), p2.astype(bf16)
            ds_ref[pair, 0], ds_ref[pair, 1] = d1.astype(bf16), d2.astype(bf16)
            p0_ref[pair], ds0_ref[pair] = p0, d0
            for h in range(2):
                part = slice(h * F, (h + 1) * F)
                y1 = jnp.where(below, d1[:, part], d2[:, part])
                y2 = jnp.where(below, d2[:, part], d1[:, part])
                for y, spot in ((y1, 2 * pair + h), (y2, H + 2 * pair + h)):
                    total_y = y[:8]
                    for k in range(1, 16):
                        total_y = total_y + pltpu.roll(y[8 * k : 8 * k + 8], F - 8 * k, 1)
                    acc_ref[spot] = total_y

    @pl.when(info[2] == 1)
    def _():
        run(a_ref, b_ref)

    @pl.when(info[2] == 0)
    def _():
        run(b_ref, a_ref)

    summed = acc_ref[:, 0, :]
    for s in range(1, 8):
        summed = summed + pltpu.roll(acc_ref[:, s, :], F - s, 1)
    turned = flip(summed)
    head = lax.broadcasted_iota(jnp.int32, (H, F), 0)
    at = lax.broadcasted_iota(jnp.int32, (H, F), 1)
    edges = ds0_ref[:, 0, :]
    zed = jnp.concatenate(
        [
            jnp.sum(edges[pair : pair + 1, h * F : (h + 1) * F], axis=1, keepdims=True)
            for pair in range(PAIRS)
            for h in range(2)
        ],
        axis=0,
    )
    one, two = turned[:H], turned[H:]
    last = jnp.sum(jnp.where(head == at, two[:, :1], 0.0), axis=0, keepdims=True)
    packed = jnp.concatenate(
        [
            jnp.where(at == 0, zed, one),
            jnp.where(at == 0, one[:, :1], two),
            jnp.broadcast_to(last, (ROWS - 2 * H, F)),
        ],
        axis=0,
    ).astype(bf16)
    for i in range(gb_ref.shape[0]):
        gb_ref[i] = packed


def unfolded(pair_ref, edge_ref, pair, below2, on2):
    folded = pair_ref[pair, 0]
    zero = jnp.zeros_like(folded)
    edge = jnp.broadcast_to(edge_ref[pair], folded.shape).astype(bf16)
    before = jnp.where(below2, folded, jnp.where(on2, edge, zero))
    return before, jnp.where(below2, zero, folded)


def sides_kernel(
    length_ref, q_hbm, g_hbm, p_ref, ds_ref, p0_ref, ds0_ref, da_ref, db_ref, held, sem,
):
    fetch((q_hbm, g_hbm), [held.at[i] for i in range(2)], sem)
    info = position(length_ref)
    row, lane = grids()
    below2, on2 = twice(lane < row), twice(lane == row)

    def run(*refs):
        for pair in range(PAIRS):
            at = pl.ds(pair * F, F)
            q2, g2 = stacked(info, held[0, :, at], held[1, :, at])
            dk = dot(jnp.concatenate(unfolded(ds_ref, ds0_ref, pair, below2, on2), axis=0), q2)
            dv = dot(jnp.concatenate(unfolded(p_ref, p0_ref, pair, below2, on2), axis=0), g2)
            for i, ref in enumerate(refs):
                ref[0, :, at] = dk[i * F : (i + 1) * F].astype(bf16)
                ref[1, :, at] = dv[i * F : (i + 1) * F].astype(bf16)

    @pl.when(info[2] == 1)
    def _():
        run(da_ref, db_ref)

    @pl.when(info[2] == 0)
    def _():
        run(db_ref, da_ref)


def outputs_kernel(
    length_ref, q_hbm, g_hbm, k_hbm, v_hbm, a_hbm, b_hbm,
    p_ref, ds_ref, p0_ref, ds0_ref, fa_ref, fb_ref,
    ctx_ref, dq_ref, gk_ref, gv_ref, held, qg_ref, sem,
):
    info = position(length_ref)
    odd = info[2]
    fetch(
        (q_hbm, g_hbm, k_hbm, v_hbm, a_hbm, b_hbm),
        [qg_ref.at[0], qg_ref.at[1], held.at[1, 0], held.at[1, 1]]
        + [held.at[2 - 2 * odd], held.at[2 * odd]],
        sem,
    )
    row, lane = grids()
    below2, on2 = twice(lane < row), twice(lane == row)
    valid = info[0] + row < info[1]
    for pair in range(PAIRS):
        at = pl.ds(pair * F, F)
        q2, g2 = stacked(info, qg_ref[0, :, at], qg_ref[1, :, at])
        p, ds = p_ref[pair, 1], ds_ref[pair, 1]
        for i, (own, out) in enumerate(((dot(ds, q2), gk_ref), (dot(p, g2), gv_ref))):
            total = own + fa_ref[i, :, at].astype(f32) + fb_ref[i, :, at].astype(f32)
            out[:, at] = total.astype(bf16)
        p_before, p_after = unfolded(p_ref, p0_ref, pair, below2, on2)
        ds_before, ds_after = unfolded(ds_ref, ds0_ref, pair, below2, on2)
        keys = jnp.concatenate([held[i, 0, :, at] for i in range(3)], axis=0)
        values = jnp.concatenate([held[i, 1, :, at] for i in range(3)], axis=0)
        ctx_t = dot(jnp.transpose(values), jnp.concatenate([p_before, p, p_after], axis=0))
        dq_t = dot(jnp.transpose(keys), jnp.concatenate([ds_before, ds, ds_after], axis=0))
        ctx = jnp.transpose(jnp.concatenate([ctx_t[:HD, :F], ctx_t[HD:, F:]], axis=0))
        ctx_ref[:, at] = jnp.where(valid, ctx, 0.0).astype(bf16)
        dq = jnp.transpose(jnp.concatenate([dq_t[:HD, :F], dq_t[HD:, F:]], axis=0))
        dq_ref[:, at] = (dq * SCALE).astype(bf16)


def fetch(sources, targets, sem):
    copies = [
        pltpu.make_async_copy(source, target, sem.at[i])
        for i, (source, target) in enumerate(zip(sources, targets))
    ]
    for copy in copies:
        copy.start()
    for copy in copies:
        copy.wait()


def stack_kernel(k_hbm, v_hbm, out_ref, sem):
    fetch((k_hbm, v_hbm), (out_ref.at[0], out_ref.at[1]), sem)


def stack(k, v):
    return pl.pallas_call(
        stack_kernel,
        in_specs=[pl.BlockSpec(memory_space=pltpu.HBM)] * 2,
        out_specs=pl.BlockSpec(memory_space=pltpu.VMEM),
        out_shape=shape(bf16, 2, F, D),
        scratch_shapes=[pltpu.SemaphoreType.DMA((2,))],
        compiler_params=pltpu.CompilerParams(vmem_limit_bytes=1 << 20),
        name="stack",
    )(k, v)


def in_vmem(kernel, far, args, out_shape, scratch, flops):
    vmem = pl.BlockSpec(memory_space=pltpu.VMEM)
    hbm = pl.BlockSpec(memory_space=pltpu.HBM)
    return pl.pallas_call(
        kernel,
        in_specs=[pl.BlockSpec(memory_space=pltpu.SMEM)]
        + [hbm] * far
        + [vmem] * (len(args) - 1 - far),
        out_specs=[vmem] * len(out_shape),
        out_shape=out_shape,
        scratch_shapes=scratch,
        compiler_params=pltpu.CompilerParams(vmem_limit_bytes=16 << 20),
        cost_estimate=pl.CostEstimate(flops=flops, bytes_accessed=4 << 20, transcendentals=0),
    )(*args)


def shape(dtype, *dims):
    return jax.ShapeDtypeStruct(dims, dtype)


def own_part(*args):
    return in_vmem(
        own_kernel, 3, args,
        [shape(f32, PAIRS, F, 2 * F)] * 3
        + [shape(f32, PAIRS, 1, 2 * F)]
        + [shape(bf16, PAIRS, 2 * F, F)] * 2,
        [
            pltpu.VMEM((3, H, F), f32),
            pltpu.VMEM((H, 2 * W + 1), f32),
            pltpu.VMEM((2, F, D), bf16),
            pltpu.SemaphoreType.DMA((3,)),
        ],
        1 << 30,
    )


def row_part(copies, *args):
    return in_vmem(
        rows_kernel, 0, args,
        [shape(bf16, PAIRS, 2, F, 2 * F)] * 2
        + [shape(f32, PAIRS, 1, 2 * F)] * 2
        + [shape(bf16, copies, ROWS, F)],
        [pltpu.VMEM((2 * H, 8, F), f32)], 1 << 30,
    )


def side_part(*args):
    return in_vmem(
        sides_kernel, 2, args,
        [shape(bf16, 2, F, D)] * 2,
        [pltpu.VMEM((2, F, D), bf16), pltpu.SemaphoreType.DMA((2,))], 1 << 30,
    )


def output_part(*args):
    return in_vmem(
        outputs_kernel, 6, args,
        [shape(bf16, F, D)] * 4,
        [
            pltpu.VMEM((3, 2, F, D), bf16),
            pltpu.VMEM((2, F, D), bf16),
            pltpu.SemaphoreType.DMA((6,)),
        ],
        1 << 30,
    )


def size_of(axes):
    count = 1
    for axis in axes:
        count *= lax.axis_size(axis)
    return count


def exchange(x, axes, head):
    count = size_of(axes)
    groups = [[(i + head) % count for i in range(count)]]
    return lax.all_to_all(x, axes, 0, 0, axis_index_groups=groups, tiled=True)


def step(query_proj, key_proj, value_proj, cotangent, lengths, rel_bias):
    ends = size_of(TM)
    near = [(i, i ^ 1) for i in range(ends)]
    far = [(i, i + 1 if i % 2 else i - 1) for i in range(1, ends - 1)]
    stay = lambda x: pltpu.with_memory_space_constraint(x, pltpu.HBM)
    q, k, v, g = (stay(x[0]) for x in (query_proj, key_proj, value_proj, cotangent))
    table = stay(rel_bias)
    kv = stack(k, v)
    side_b = lax.ppermute(kv, TM, far)
    side_a = lax.ppermute(kv, TM, near)
    s, gp, bias, edge, q2, g2 = own_part(lengths, q, g, table, kv)
    p, ds, p0, ds0, gb = row_part(size_of(XY), lengths, side_a, side_b, s, gp, bias, edge, q2, g2)
    z = exchange(gb, XY, HEAD_XY)
    da, db = side_part(lengths, q, g, p, ds, p0, ds0)
    fb = lax.ppermute(db, TM, far)
    fa = lax.ppermute(da, TM, near)
    z = jnp.sum(z.astype(f32), axis=0).astype(bf16)
    z = jnp.broadcast_to(z[None], (size_of(Z16), ROWS, F))
    z = exchange(z, Z16, HEAD_Z)
    ctx, dq, grad_key, grad_value = output_part(
        lengths, q, g, k, v, stay(side_a), stay(side_b), p, ds, p0, ds0, fa, fb
    )
    z = jnp.sum(z.astype(f32), axis=0)
    grad_bias = jnp.concatenate([z[:H], z[H : 2 * H], z[2 * H, :H, None]], axis=1)
    return ctx[None], dq[None], grad_key[None], grad_value[None], grad_bias


def solution(mesh):
    finer = Mesh(mesh.devices.reshape(2, 4, 8, 4, 2), AXES)
    in_specs = (P(DP, TM, None), P(DP, TM, None), P(DP, TM, None), P(DP, TM, None), P(DP), P())
    out_specs = (P(DP, TM, None), P(DP, TM, None), P(DP, TM, None), P(DP, TM, None), P())
    return jax.shard_map(step, mesh=finer, in_specs=in_specs, out_specs=out_specs, check_vma=False)
```
